32 devices in a mesh: src: 8 (over y, x, core), rcv: 4 (over z).
Axes of the slice: x: 2, y: 2, z: 4, core: 2. Of those that a mesh axis runs over, the one named last changes fastest.
Arguments:
- traces: bfloat16 [256, 128, 512], P('src', 'rcv')
- block_recorded_mask: int32 [8, 4], P('src', 'rcv'), may hold values 0 or 1
- block_live_count: int32 [8, 4], P('src', 'rcv'), may hold values from 256 to 1024, as said below
Outputs:
- deconvolved: float32 [256, 128, 512], P('src', 'rcv')
The draws below stay inside these ranges and needn't reach their ends.
Inputs may be any that keep to these rules, and one draw needn't show every extreme that they name: `block_live_count`: every block's count lies between a quarter of its 1024 traces and all of them; some block is full in every draw.
All inputs are finite; a program needn't handle non-finite values. No bound on the sum of `block_recorded_mask` on one device may be relied on, other than what follows from the above.
Results may differ from the reference program's by a relative error of at most 0.0003.
Values sent between devices are 32-bit elements; how exact they have to be, the bound alone decides.
A program may use at most 64 MiB of HBM per device.

```python
import math
import jax
import jax.numpy as jnp
from jax import lax

NT = 512
NF = 256
SRC_DEV = 32
BLOCK_RECEIVERS = 32
ITERS = 2
NBS = 8
NBR = 4
NS = 256
NR = 128


def draw_traces(key, part):
    noise_key, src_key, rcv_key = jax.random.split(key, 3)
    shape = (NS, NR, NT)
    noise = jax.random.normal(noise_key, shape, jnp.float32)
    low, high = (math.log(0.3), math.log(3.0))
    src_gain = jnp.exp(jax.random.uniform(src_key, (NS,), jnp.float32, low, high))
    rcv_gain = jnp.exp(jax.random.uniform(rcv_key, (NR,), jnp.float32, low, high))
    return (noise * src_gain[:, None, None] * rcv_gain[None, :, None]).astype(jnp.bfloat16)


def draw_block_live_count(key, part):
    count_key, place_key = jax.random.split(jax.random.fold_in(key, 7))
    full = SRC_DEV * BLOCK_RECEIVERS
    counts = jax.random.randint(count_key, (NBS * NBR,), full // 4, 2 * full, jnp.int32)
    counts = jnp.minimum(counts, full)
    place = jax.random.randint(place_key, (), 0, NBS * NBR, jnp.int32)
    counts = jnp.where(jnp.arange(NBS * NBR, dtype=jnp.int32) == place, full, counts)
    return counts.reshape(NBS, NBR).astype(jnp.int32)


def place_ends(values, stream_key, smallest, largest):
    longest = values.shape.index(max(values.shape))
    spots = []
    for shift in (0, 1):
        where = [jax.random.randint(jax.random.fold_in(stream_key, axis), (), 0, length) for axis, length in enumerate(values.shape)]
        where[longest] = (where[longest] + shift) % values.shape[longest]
        spots.append(tuple(where))
    return values.at[spots[0]].set(smallest).at[spots[1]].set(largest)


def setup_inputs(seed: int = 0) -> dict:
    key_of = jax.random.split(jax.random.key(seed), 4)
    return {
        "traces": draw_traces(jax.random.fold_in(key_of[3], 71), 0),
        "block_recorded_mask": place_ends((jax.random.randint(key_of[1], (NBS, NBR), 0, 4) < 3).astype(jnp.int32), jax.random.fold_in(key_of[1], 1), 0, 1),
        "block_live_count": draw_block_live_count(jax.random.fold_in(key_of[3], 71), 0),
    }


WATER = 0.01


def log_power(real_part, imag_part):
    power = (real_part * real_part + imag_part * imag_part) / NT
    level = jnp.mean(power, axis=-1, keepdims=True)
    return jnp.log(power + WATER * level + 1e-6)


def robust_weights(logs, trace_present, src_term, rcv_term):
    resid = logs - src_term[:, None, :] - rcv_term[None, :, :]
    square = resid * resid
    padded_spectra = jnp.pad(square, ((0, 0), (0, 0), (1, 1)), mode="edge")
    smooth = 0.25 * padded_spectra[..., :-2] + 0.5 * square + 0.25 * padded_spectra[..., 2:]
    return trace_present[:, :, None] / (1.0 + smooth)


def trace_presence(block_recorded_mask, block_live_count):
    local = (jnp.arange(SRC_DEV)[:, None] * BLOCK_RECEIVERS + jnp.arange(BLOCK_RECEIVERS)[None, :]).astype(jnp.int32)
    trace_present = (local[None, :, None, :] < block_live_count[:, None, :, None]) & (block_recorded_mask[:, None, :, None] == 1)
    return trace_present.reshape(NS, NR).astype(jnp.float32)


def reference(traces, block_recorded_mask, block_live_count):
    trace_present = trace_presence(block_recorded_mask, block_live_count)
    blocks = traces.reshape(NBS, SRC_DEV, NR, NT)
    alive_blocks = trace_present.reshape(NBS, SRC_DEV, NR)

    def spectra_of(block):
        spectrum = jnp.fft.rfft(block.astype(jnp.float32), axis=-1)[..., :NF]
        return log_power(jnp.real(spectrum), jnp.imag(spectrum))

    logs = lax.map(spectra_of, blocks)
    src_term = jnp.zeros((NBS, SRC_DEV, NF), jnp.float32)
    rcv_term = jnp.zeros((NR, NF), jnp.float32)
    for sweep in range(ITERS):
        def visit(carry, item, rcv_term=rcv_term):
            log_blk, alive_blk, src_blk = item
            weight = robust_weights(log_blk, alive_blk, src_blk, rcv_term)
            new_src = jnp.sum(weight * (log_blk - rcv_term[None]), axis=1) / (jnp.sum(weight, axis=1) + 1.0)
            carry = (carry[0] + jnp.sum(weight * (log_blk - src_blk[:, None, :]), axis=0),
                     carry[1] + jnp.sum(weight, axis=0))
            return carry, new_src

        start = (jnp.zeros((NR, NF), jnp.float32), jnp.zeros((NR, NF), jnp.float32))
        (weighted, summed_weights), src_term = lax.scan(visit, start, (logs, alive_blocks, src_term))
        rcv_term = weighted / (summed_weights + 1.0)

    def apply_filters(item):
        block, src_blk, alive_blk = item
        spectrum = jnp.fft.rfft(block.astype(jnp.float32), axis=-1)
        gain = jnp.exp(-0.5 * (src_blk[:, None, :] + rcv_term[None, :, :]))
        gain = jnp.concatenate([gain, jnp.zeros(gain.shape[:-1] + (1,), gain.dtype)], axis=-1)
        return jnp.fft.irfft(spectrum * gain, n=NT, axis=-1) * alive_blk[..., None]

    result = lax.map(apply_filters, (blocks, src_term, alive_blocks))
    return result.reshape(NS, NR, NT)
```

```python
import functools
import math

import jax
import jax.numpy as jnp
import numpy as np
from jax import lax
from jax.experimental import pallas as pl
from jax.experimental.pallas import tpu as pltpu
from jax.sharding import PartitionSpec as P

ITERS = 2
WATER = 0.01
LANES = 128
MESH = pl.DeviceIdType.MESH
F32 = jnp.float32
BF16 = jnp.bfloat16


def log_power(real_part, imag_part, length):
    power = (real_part * real_part + imag_part * imag_part) / length
    level = jnp.mean(power, axis=-1, keepdims=True)
    return jnp.log(power + WATER * level + 1e-06)


def robust_weights(logs, trace_present, src_term, rcv_term):
    resid = logs - src_term[:, None, :] - rcv_term[None, :, :]
    square = resid * resid
    padded_spectra = jnp.pad(square, ((0, 0), (0, 0), (1, 1)), mode="edge")
    smooth = 0.25 * padded_spectra[..., :-2] + 0.5 * square + 0.25 * padded_spectra[..., 2:]
    return trace_present[:, :, None] / (1.0 + smooth)


def transform_tables(length, freqs):
    sample = lax.iota(jnp.int32, length)
    bins = lax.iota(jnp.int32, freqs)
    phase = sample[:, None] * bins[None, :] % length
    angle = phase.astype(jnp.float32) * (2.0 * math.pi / length)
    cosine = jnp.cos(angle)
    sine = jnp.sin(angle)
    forward = jnp.concatenate([cosine, -sine], axis=1)
    weight_factor = jnp.where(bins == 0, 1.0, 2.0).astype(jnp.float32) / length
    inverse = jnp.concatenate(
        [cosine.T * weight_factor[:, None], -sine.T * weight_factor[:, None]], axis=0
    )
    forward_high = forward.astype(jnp.bfloat16)
    widened = lax.optimization_barrier(forward_high).astype(jnp.float32)
    forward_low = (forward - widened).astype(jnp.bfloat16)
    return (forward_high, forward_low, inverse)


def plain_body(traces, block_recorded_mask, block_live_count):
    src_rows, rcv_rows, length = traces.shape
    freqs = length // 2
    count = src_rows * rcv_rows
    forward_high, forward_low, inverse = transform_tables(length, freqs)
    local = lax.iota(jnp.int32, count).reshape(src_rows, rcv_rows)
    recorded = block_recorded_mask[0, 0] == 1
    trace_present = ((local < block_live_count[0, 0]) & recorded).astype(jnp.float32)
    flat = traces.reshape(count, length)
    upper = jnp.dot(flat, forward_high, preferred_element_type=jnp.float32)
    spectra = upper + jnp.dot(flat, forward_low, preferred_element_type=jnp.float32)
    real_part = spectra[:, :freqs]
    imag_part = spectra[:, freqs:]
    logs = log_power(real_part, imag_part, length).reshape(src_rows, rcv_rows, freqs)
    src_term = jnp.zeros((src_rows, freqs), jnp.float32)
    rcv_term = jnp.zeros((rcv_rows, freqs), jnp.float32)
    for sweep in range(ITERS):
        weight = robust_weights(logs, trace_present, src_term, rcv_term)
        src_weighted, src_total = lax.psum(
            (jnp.sum(weight * (logs - rcv_term[None, :, :]), axis=1), jnp.sum(weight, axis=1)),
            "rcv",
        )
        rcv_weighted = jnp.sum(weight * (logs - src_term[:, None, :]), axis=0)
        rcv_total = jnp.sum(weight, axis=0)
        summed, totals = lax.psum((rcv_weighted, rcv_total), "src")
        new_rcv = summed / (totals + 1.0)
        src_term = src_weighted / (src_total + 1.0)
        rcv_term = new_rcv
    gain = jnp.exp(-0.5 * (src_term[:, None, :] + rcv_term[None, :, :])).reshape(count, freqs)
    filtered = jnp.concatenate([real_part * gain, imag_part * gain], axis=1)
    output = jnp.dot(
        filtered, inverse, precision=lax.Precision.HIGH, preferred_element_type=jnp.float32
    )
    return output.reshape(src_rows, rcv_rows, length) * trace_present[:, :, None]


def split_table(table):
    table = table.astype(np.float32)
    high = table.astype(BF16)
    low = (table - high.astype(np.float32)).astype(BF16)
    return high, low


def kernel_tables(length):
    half = length // 2
    sample = np.arange(length)
    forward, inverse = [], []
    for parity in (0, 1):
        bins = np.arange(parity, half, 2)
        angle = (sample[:, None] * bins[None, :] % length) * (2.0 * math.pi / length)
        cosine, sine = np.cos(angle), np.sin(angle)
        forward += [cosine, -sine]
        factor = np.where(bins == 0, 1.0, 2.0)[:, None] / length
        inverse.append(np.concatenate([cosine[:half].T * factor, -sine[:half].T * factor], axis=0))
    return split_table(np.concatenate(forward, axis=1)) + split_table(np.stack(inverse))


def weigh(even, odd, present, first, last):
    even, odd = even * even, odd * odd
    quarter = even.shape[1]
    left = jnp.where(first, even, pltpu.roll(odd, 1, 1))
    right = jnp.where(last, odd, pltpu.roll(even, quarter - 1, 1))
    smooth_even = 0.25 * left + 0.5 * even + 0.25 * odd
    smooth_odd = 0.25 * even + 0.5 * odd + 0.25 * right
    return present / (1.0 + smooth_even), present / (1.0 + smooth_odd)


def sweep_kernel(
    rows, ns, nr, mask_ref, count_ref, x_ref, high_ref, low_ref,
    spec_ref, src_ref, rcv_ref,
    logs, acc, s_part, r_part, s_recv, r_recv, s_gath, r_gath,
    s_ssem, s_rsem, r_ssem, r_rsem, sg_ssem, sg_rsem, rg_ssem, rg_rsem,
):
    src_rows, rcv_rows = rows
    length = x_ref.shape[1]
    quarter = length // 4
    half = length // 2
    ks, kr = src_rows // nr, rcv_rows // ns
    tile = ks * rcv_rows
    me_s, me_r = lax.axis_index("src"), lax.axis_index("rcv")

    barrier = pltpu.get_barrier_semaphore()
    for d in range(1, ns):
        pl.semaphore_signal(barrier, inc=1, device_id={"src": lax.rem(me_s + d, ns)}, device_id_type=MESH)
    for d in range(1, nr):
        pl.semaphore_signal(barrier, inc=1, device_id={"rcv": lax.rem(me_r + d, nr)}, device_id_type=MESH)

    limit = count_ref[0, 0] * jnp.where(mask_ref[0, 0] == 1, 1, 0)
    shape = (rcv_rows, quarter)
    row = lax.broadcasted_iota(jnp.int32, shape, 0)
    lane = lax.broadcasted_iota(jnp.int32, shape, 1)
    first, last = lane == 0, lane == quarter - 1

    def scatter(it, axis, n, me, part, recv, ssem, rsem):
        copies = []
        for d in range(1, n):
            peer = lax.rem(me + d, n)
            copy = pltpu.make_async_remote_copy(
                src_ref=part.at[it, peer], dst_ref=recv.at[it, me],
                send_sem=ssem.at[it, d], recv_sem=rsem.at[it, me],
                device_id={axis: peer}, device_id_type=MESH,
            )
            copy.start()
            copies.append(copy)
        return copies

    def gather(it, axis, n, me, gath, ssem, rsem):
        copies = []
        for d in range(1, n):
            peer = lax.rem(me + d, n)
            copy = pltpu.make_async_remote_copy(
                src_ref=gath.at[it, me], dst_ref=gath.at[it, me],
                send_sem=ssem.at[it, d], recv_sem=rsem.at[it, me],
                device_id={axis: peer}, device_id_type=MESH,
            )
            copy.start()
            copies.append(copy)
        return copies

    def arrive(it, axis, n, me, buf, ssem, rsem):
        for d in range(1, n):
            peer = lax.rem(me + d, n)
            pltpu.make_async_remote_copy(
                src_ref=buf.at[it, peer], dst_ref=buf.at[it, peer],
                send_sem=ssem.at[it, d], recv_sem=rsem.at[it, peer],
                device_id={axis: peer}, device_id_type=MESH,
            ).wait_recv()

    def finish(it, n, me, k, part, recv, gath):
        recv[it, me] = part[it, me]
        total = recv[it, 0]
        for j in range(1, n):
            total = total + recv[it, j]
        gath[it, me] = total[:k] / (total[k:] + 1.0)

    sends = []
    acc[...] = jnp.zeros_like(acc)
    for it in range(ITERS):
        def chunk(c, carry, it=it):
            base = pl.multiple_of(c * tile, tile)
            if it == 0:
                x = x_ref[pl.ds(base, tile), :]
                spec_ref[pl.ds(base, tile), :] = jnp.dot(
                    x, high_ref[...], preferred_element_type=F32
                ) + jnp.dot(x, low_ref[...], preferred_element_type=F32)
            else:
                terms = src_ref[pl.ds(pl.multiple_of(c * ks, ks), ks), :]
            sums = [jnp.zeros(shape, F32) for _ in range(4)]
            for i in range(ks):
                at = pl.ds(pl.multiple_of(base + i * rcv_rows, rcv_rows), rcv_rows)
                present = jnp.where(row + (base + i * rcv_rows) < limit, 1.0, 0.0)
                if it == 0:
                    powers = []
                    for parity in (0, 1):
                        re = spec_ref[at, parity * half : parity * half + quarter]
                        im = spec_ref[at, parity * half + quarter : (parity + 1) * half]
                        powers.append((re * re + im * im) * (1.0 / length))
                    level = jnp.sum(powers[0] + powers[1], axis=1, keepdims=True) * (1.0 / half)
                    floor = WATER * level + 1e-06
                    even, odd = jnp.log(powers[0] + floor), jnp.log(powers[1] + floor)
                    logs[at, :quarter] = even
                    logs[at, quarter:] = odd
                    we, wo = weigh(even, odd, present, first, last)
                    src_even = rcv_even = we * even
                    src_odd = rcv_odd = wo * odd
                else:
                    even, odd = logs[at, :quarter], logs[at, quarter:]
                    ue, uo = even - terms[i : i + 1, :quarter], odd - terms[i : i + 1, quarter:]
                    te, to = rcv_ref[:, :quarter], rcv_ref[:, quarter:]
                    we, wo = weigh(ue - te, uo - to, present, first, last)
                    src_even, src_odd = we * (even - te), wo * (odd - to)
                    rcv_even, rcv_odd = we * ue, wo * uo
                s_part[it, c, i : i + 1, :quarter] = jnp.sum(src_even, axis=0, keepdims=True)
                s_part[it, c, i : i + 1, quarter:] = jnp.sum(src_odd, axis=0, keepdims=True)
                s_part[it, c, ks + i : ks + i + 1, :quarter] = jnp.sum(we, axis=0, keepdims=True)
                s_part[it, c, ks + i : ks + i + 1, quarter:] = jnp.sum(wo, axis=0, keepdims=True)
                for q, value in enumerate((rcv_even, rcv_odd, we, wo)):
                    sums[q] = sums[q] + value
            acc[it, 0, :, :quarter] += sums[0]
            acc[it, 0, :, quarter:] += sums[1]
            acc[it, 1, :, :quarter] += sums[2]
            acc[it, 1, :, quarter:] += sums[3]
            return carry

        lax.fori_loop(0, nr, chunk, 0)
        for p in range(ns):
            r_part[it, p, :kr, :] = acc[it, 0, p * kr : (p + 1) * kr, :]
            r_part[it, p, kr:, :] = acc[it, 1, p * kr : (p + 1) * kr, :]
        if it == 0:
            pl.semaphore_wait(barrier, ns + nr - 2)
        sends += scatter(it, "rcv", nr, me_r, s_part, s_recv, s_ssem, s_rsem)
        sends += scatter(it, "src", ns, me_s, r_part, r_recv, r_ssem, r_rsem)
        arrive(it, "src", ns, me_s, r_recv, r_ssem, r_rsem)
        finish(it, ns, me_s, kr, r_part, r_recv, r_gath)
        sends += gather(it, "src", ns, me_s, r_gath, rg_ssem, rg_rsem)
        arrive(it, "rcv", nr, me_r, s_recv, s_ssem, s_rsem)
        finish(it, nr, me_r, ks, s_part, s_recv, s_gath)
        sends += gather(it, "rcv", nr, me_r, s_gath, sg_ssem, sg_rsem)
        arrive(it, "src", ns, me_s, r_gath, rg_ssem, rg_rsem)
        for p in range(ns):
            rcv_ref[p * kr : (p + 1) * kr, :] = r_gath[it, p]
        arrive(it, "rcv", nr, me_r, s_gath, sg_ssem, sg_rsem)
        for p in range(nr):
            src_ref[p * ks : (p + 1) * ks, :] = s_gath[it, p]
    for copy in sends:
        copy.wait_send()


def filter_kernel(
    rows, mask_ref, count_ref, spec_ref, src_ref, rcv_ref, high_ref, low_ref, out_ref, upper, lower
):
    rcv_rows, quarter = rows[1], spec_ref.shape[1] // 4
    half = 2 * quarter
    sources = spec_ref.shape[0] // rcv_rows
    base = pl.program_id(0) * spec_ref.shape[0]
    limit = count_ref[0, 0] * jnp.where(mask_ref[0, 0] == 1, 1, 0)
    row = lax.broadcasted_iota(jnp.int32, (rcv_rows, quarter), 0)
    for i in range(sources):
        at = slice(i * rcv_rows, (i + 1) * rcv_rows)
        alive = row + (base + i * rcv_rows) < limit
        for parity in (0, 1):
            cols = slice(parity * quarter, (parity + 1) * quarter)
            gain = jnp.exp(-0.5 * (src_ref[i : i + 1, cols] + rcv_ref[:, cols]))
            gain = jnp.where(alive, gain, 0.0)
            for part in (0, 1):
                lo = parity * half + part * quarter
                value = spec_ref[at, lo : lo + quarter] * gain
                high = value.astype(BF16)
                upper[at, lo : lo + quarter] = high
                lower[at, lo : lo + quarter] = (value - high.astype(F32)).astype(BF16)

    def product(parity):
        cols = slice(parity * half, (parity + 1) * half)
        big, small = upper[:, cols], lower[:, cols]
        dot = functools.partial(jnp.dot, preferred_element_type=F32)
        return dot(big, high_ref[parity]) + (dot(small, high_ref[parity]) + dot(big, low_ref[parity]))

    a, b = product(0), product(1)
    out_ref[:, :half] = a + b
    out_ref[:, half:] = a - b


def kernel_body(ns, nr, traces, mask, count):
    src_rows, rcv_rows, length = traces.shape
    total, half = src_rows * rcv_rows, length // 2
    ks, kr = src_rows // nr, rcv_rows // ns
    forward_high, forward_low, inverse_high, inverse_low = kernel_tables(length)
    flat = traces.reshape(total, length)
    vmem = pl.BlockSpec(memory_space=pltpu.VMEM)
    smem = pl.BlockSpec(memory_space=pltpu.SMEM)
    dma = pltpu.SemaphoreType.DMA
    spectra, src_term, rcv_term = pl.pallas_call(
        functools.partial(sweep_kernel, (src_rows, rcv_rows), ns, nr),
        out_shape=(
            jax.ShapeDtypeStruct((total, length), F32),
            jax.ShapeDtypeStruct((src_rows, half), F32),
            jax.ShapeDtypeStruct((rcv_rows, half), F32),
        ),
        in_specs=[smem, smem, vmem, vmem, vmem],
        out_specs=(vmem, vmem, vmem),
        scratch_shapes=[
            pltpu.VMEM((total, half), F32),
            pltpu.VMEM((ITERS, 2, rcv_rows, half), F32),
            pltpu.VMEM((ITERS, nr, 2 * ks, half), F32),
            pltpu.VMEM((ITERS, ns, 2 * kr, half), F32),
            pltpu.VMEM((ITERS, nr, 2 * ks, half), F32),
            pltpu.VMEM((ITERS, ns, 2 * kr, half), F32),
            pltpu.VMEM((ITERS, nr, ks, half), F32),
            pltpu.VMEM((ITERS, ns, kr, half), F32),
            dma((ITERS, nr)), dma((ITERS, nr)), dma((ITERS, ns)), dma((ITERS, ns)),
            dma((ITERS, nr)), dma((ITERS, nr)), dma((ITERS, ns)), dma((ITERS, ns)),
        ],
        compiler_params=pltpu.CompilerParams(
            collective_id=0, has_side_effects=True, vmem_limit_bytes=24 * 1024 * 1024
        ),
        name="sweeps",
    )(mask, count, flat, jnp.asarray(forward_high), jnp.asarray(forward_low))
    tile = ks * rcv_rows
    output = pl.pallas_call(
        functools.partial(filter_kernel, (src_rows, rcv_rows)),
        grid=(nr,),
        out_shape=jax.ShapeDtypeStruct((total, length), F32),
        in_specs=[
            smem,
            smem,
            pl.BlockSpec((tile, length), lambda i: (i, 0)),
            pl.BlockSpec((ks, half), lambda i: (i, 0)),
            pl.BlockSpec((rcv_rows, half), lambda i: (0, 0)),
            pl.BlockSpec((2, half, half), lambda i: (0, 0, 0)),
            pl.BlockSpec((2, half, half), lambda i: (0, 0, 0)),
        ],
        out_specs=pl.BlockSpec((tile, length), lambda i: (i, 0)),
        scratch_shapes=[pltpu.VMEM((tile, length), BF16), pltpu.VMEM((tile, length), BF16)],
        compiler_params=pltpu.CompilerParams(vmem_limit_bytes=24 * 1024 * 1024),
        name="filters",
    )(mask, count, spectra, src_term, rcv_term, jnp.asarray(inverse_high), jnp.asarray(inverse_low))
    return output.reshape(src_rows, rcv_rows, length)


def solution(mesh):
    ns, nr = mesh.shape["src"], mesh.shape["rcv"]

    def body(traces, mask, count):
        src_rows, rcv_rows, length = traces.shape
        fits = src_rows % (8 * nr) == 0 and rcv_rows % (4 * ns) == 0 and length % (4 * LANES) == 0
        if fits and ns > 1 and nr > 1:
            return kernel_body(ns, nr, traces, mask, count)
        return plain_body(traces, mask, count)

    return jax.shard_map(
        body,
        mesh=mesh,
        in_specs=(P("src", "rcv", None), P("src", "rcv"), P("src", "rcv")),
        out_specs=P("src", "rcv", None),
        check_vma=False,
    )
```

```python
import functools
import math

import jax
import jax.numpy as jnp
import numpy as np
from jax import lax
from jax.experimental import pallas as pl
from jax.experimental.pallas import tpu as pltpu
from jax.sharding import PartitionSpec as P

ITERS = 2
WATER = 0.01
LANES = 128
VMEM_BYTES = 64 * 1024 * 1024
ROOM = 44 * 256 * 1024
MESH = pl.DeviceIdType.MESH
F32 = jnp.float32
BF16 = jnp.bfloat16


def log_power(real_part, imag_part, length):
    power = (real_part * real_part + imag_part * imag_part) / length
    level = jnp.mean(power, axis=-1, keepdims=True)
    return jnp.log(power + WATER * level + 1e-06)


def robust_weights(logs, trace_present, src_term, rcv_term):
    resid = logs - src_term[:, None, :] - rcv_term[None, :, :]
    square = resid * resid
    padded_spectra = jnp.pad(square, ((0, 0), (0, 0), (1, 1)), mode="edge")
    smooth = 0.25 * padded_spectra[..., :-2] + 0.5 * square + 0.25 * padded_spectra[..., 2:]
    return trace_present[:, :, None] / (1.0 + smooth)


def transform_tables(length, freqs):
    sample = lax.iota(jnp.int32, length)
    bins = lax.iota(jnp.int32, freqs)
    phase = sample[:, None] * bins[None, :] % length
    angle = phase.astype(jnp.float32) * (2.0 * math.pi / length)
    cosine = jnp.cos(angle)
    sine = jnp.sin(angle)
    forward = jnp.concatenate([cosine, -sine], axis=1)
    weight_factor = jnp.where(bins == 0, 1.0, 2.0).astype(jnp.float32) / length
    inverse = jnp.concatenate(
        [cosine.T * weight_factor[:, None], -sine.T * weight_factor[:, None]], axis=0
    )
    forward_high = forward.astype(jnp.bfloat16)
    widened = lax.optimization_barrier(forward_high).astype(jnp.float32)
    forward_low = (forward - widened).astype(jnp.bfloat16)
    return (forward_high, forward_low, inverse)


def plain_body(traces, block_recorded_mask, block_live_count):
    src_rows, rcv_rows, length = traces.shape
    freqs = length // 2
    count = src_rows * rcv_rows
    forward_high, forward_low, inverse = transform_tables(length, freqs)
    local = lax.iota(jnp.int32, count).reshape(src_rows, rcv_rows)
    recorded = block_recorded_mask[0, 0] == 1
    trace_present = ((local < block_live_count[0, 0]) & recorded).astype(jnp.float32)
    flat = traces.reshape(count, length)
    upper = jnp.dot(flat, forward_high, preferred_element_type=jnp.float32)
    spectra = upper + jnp.dot(flat, forward_low, preferred_element_type=jnp.float32)
    real_part = spectra[:, :freqs]
    imag_part = spectra[:, freqs:]
    logs = log_power(real_part, imag_part, length).reshape(src_rows, rcv_rows, freqs)
    src_term = jnp.zeros((src_rows, freqs), jnp.float32)
    rcv_term = jnp.zeros((rcv_rows, freqs), jnp.float32)
    for sweep in range(ITERS):
        weight = robust_weights(logs, trace_present, src_term, rcv_term)
        src_weighted, src_total = lax.psum(
            (jnp.sum(weight * (logs - rcv_term[None, :, :]), axis=1), jnp.sum(weight, axis=1)),
            "rcv",
        )
        rcv_weighted = jnp.sum(weight * (logs - src_term[:, None, :]), axis=0)
        rcv_total = jnp.sum(weight, axis=0)
        summed, totals = lax.psum((rcv_weighted, rcv_total), "src")
        new_rcv = summed / (totals + 1.0)
        src_term = src_weighted / (src_total + 1.0)
        rcv_term = new_rcv
    gain = jnp.exp(-0.5 * (src_term[:, None, :] + rcv_term[None, :, :])).reshape(count, freqs)
    filtered = jnp.concatenate([real_part * gain, imag_part * gain], axis=1)
    output = jnp.dot(
        filtered, inverse, precision=lax.Precision.HIGH, preferred_element_type=jnp.float32
    )
    return output.reshape(src_rows, rcv_rows, length) * trace_present[:, :, None]


def split_table(table):
    table = table.astype(np.float32)
    high = table.astype(BF16)
    low = (table - high.astype(np.float32)).astype(BF16)
    return high, low


def kernel_tables(length):
    half = length // 2
    sample = np.arange(length)
    forward, inverse = [], []
    for parity in (0, 1):
        bins = np.arange(parity, half, 2)
        angle = (sample[:, None] * bins[None, :] % length) * (2.0 * math.pi / length)
        cosine, sine = np.cos(angle), np.sin(angle)
        forward += [cosine, -sine]
        factor = np.where(bins == 0, 1.0, 2.0)[:, None] / length
        inverse.append(np.concatenate([cosine[:half].T * factor, -sine[:half].T * factor], axis=0))
    return split_table(np.concatenate(forward, axis=1)) + (np.concatenate(split_table(np.stack(inverse))),)


def weigh(even, odd, present, first, last):
    even, odd = even * even, odd * odd
    quarter = even.shape[1]
    left = jnp.where(first, even, pltpu.roll(odd, 1, 1))
    right = jnp.where(last, odd, pltpu.roll(even, quarter - 1, 1))
    smooth_even = 0.25 * left + 0.5 * even + 0.25 * odd
    smooth_odd = 0.25 * even + 0.5 * odd + 0.25 * right
    return present / (1.0 + smooth_even), present / (1.0 + smooth_odd)


def far_first(me, n):
    order = []
    for d in range(n - 1):
        down, up = n - 1 - d, d
        down = down - jnp.where(down <= me, 1, 0)
        up = up + jnp.where(up >= me, 1, 0)
        order.append(jnp.where(2 * me < n, down, up))
    return order + [me]


def sweep_kernel(
    rows, ns, nr, mask_ref, count_ref, x_hbm, high_hbm, low_hbm, inv_hbm,
    spec_hbm, src_ref, rcv_ref, inv_ref,
    spec_ref, x_ref, high_ref, low_ref,
    logs, acc, s_part, r_part, s_recv, r_recv, s_gath, r_gath, in_sem, out_sem,
    s_ssem, s_rsem, r_ssem, r_rsem, sg_ssem, sg_rsem, rg_ssem, rg_rsem,
):
    src_rows, rcv_rows = rows
    length = x_ref.shape[1]
    quarter = length // 4
    half = length // 2
    ks, kr = src_rows // nr, rcv_rows // ns
    tile = ks * rcv_rows
    me_s, me_r = lax.axis_index("src"), lax.axis_index("rcv")
    order = far_first(me_r, nr)

    barrier = pltpu.get_barrier_semaphore()
    for d in range(1, nr):
        pl.semaphore_signal(barrier, inc=1, device_id={"rcv": lax.rem(me_r + d, nr)}, device_id_type=MESH)
    for d in range(1, ns):
        pl.semaphore_signal(barrier, inc=1, device_id={"src": lax.rem(me_s + d, ns)}, device_id_type=MESH)

    loads = [
        pltpu.make_async_copy(high_hbm, high_ref, in_sem.at[nr]),
        pltpu.make_async_copy(low_hbm, low_ref, in_sem.at[nr + 1]),
    ]
    for d in range(nr):
        base = pl.multiple_of(order[d] * tile, tile)
        loads.append(
            pltpu.make_async_copy(x_hbm.at[pl.ds(base, tile)], x_ref.at[d * tile : (d + 1) * tile], in_sem.at[d])
        )
    loads.append(pltpu.make_async_copy(inv_hbm, inv_ref, in_sem.at[nr + 2]))
    for d in (2, 0, 1, *range(3, nr + 3)):
        loads[d].start()

    limit = count_ref[0, 0] * jnp.where(mask_ref[0, 0] == 1, 1, 0)
    shape = (rcv_rows, quarter)
    row = lax.broadcasted_iota(jnp.int32, shape, 0)
    lane = lax.broadcasted_iota(jnp.int32, shape, 1)
    first, last = lane == 0, lane == quarter - 1
    sends, stores = [], []

    def send(it, axis, peer, slot, src, dst, ssem, rsem, me):
        copy = pltpu.make_async_remote_copy(
            src_ref=src, dst_ref=dst, send_sem=ssem.at[it, slot], recv_sem=rsem.at[it, me],
            device_id={axis: peer}, device_id_type=MESH,
        )
        copy.start()
        sends.append(copy)

    def gather(it, axis, n, me, gath, ssem, rsem):
        for d in range(1, n):
            peer = lax.rem(me + d, n)
            send(it, axis, peer, d, gath.at[it, me], gath.at[it, me], ssem, rsem, me)

    def arrive(it, axis, peer, buf, ssem, rsem):
        pltpu.make_async_remote_copy(
            src_ref=buf.at[it, peer], dst_ref=buf.at[it, peer],
            send_sem=ssem.at[it, 0], recv_sem=rsem.at[it, peer],
            device_id={axis: peer}, device_id_type=MESH,
        ).wait_recv()

    def arrive_all(it, axis, n, me, buf, ssem, rsem):
        for d in range(1, n):
            arrive(it, axis, lax.rem(me + d, n), buf, ssem, rsem)

    def finish(it, n, me, k, part, recv, gath):
        recv[it, me] = part[it, me]
        total = recv[it, 0]
        for j in range(1, n):
            total = total + recv[it, j]
        gath[it, me] = total[:k] / (total[k:] + 1.0)

    def finish_src(it):
        arrive_all(it, "rcv", nr, me_r, s_recv, s_ssem, s_rsem)
        finish(it, nr, me_r, ks, s_part, s_recv, s_gath)
        gather(it, "rcv", nr, me_r, s_gath, sg_ssem, sg_rsem)

    def finish_rcv(it):
        arrive_all(it, "src", ns, me_s, r_recv, r_ssem, r_rsem)
        finish(it, ns, me_s, kr, r_part, r_recv, r_gath)
        gather(it, "src", ns, me_s, r_gath, rg_ssem, rg_rsem)

    def collect_rcv(it):
        arrive_all(it, "src", ns, me_s, r_gath, rg_ssem, rg_rsem)
        for p in range(ns):
            rcv_ref[p * kr : (p + 1) * kr, :] = r_gath[it, p]

    def transform(d):
        loads[d + 2].wait()
        at = slice(d * tile, (d + 1) * tile)
        x = x_ref[at, :]
        spec_ref[at, :] = jnp.dot(x, high_ref[...], preferred_element_type=F32) + jnp.dot(
            x, low_ref[...], preferred_element_type=F32
        )

    loads[0].wait()
    loads[1].wait()
    transform(0)
    for it in range(ITERS):
        steps = range(nr) if it == 0 else range(nr - 1, -1, -1)
        for count, d in enumerate(steps):
            chunk = order[d]
            base = chunk * tile
            if it == 0:
                if d + 1 < nr:
                    transform(d + 1)
            else:
                if d < nr - 1:
                    arrive(it - 1, "rcv", chunk, s_gath, sg_ssem, sg_rsem)
                terms = s_gath[it - 1, chunk]
            sums = [None] * 4
            for i in range(ks):
                top = d * tile + i * rcv_rows
                at = slice(top, top + rcv_rows)
                present = jnp.where(row + (base + i * rcv_rows) < limit, 1.0, 0.0)
                if it == 0:
                    powers = []
                    for parity in (0, 1):
                        re = spec_ref[at, parity * half : parity * half + quarter]
                        im = spec_ref[at, parity * half + quarter : (parity + 1) * half]
                        powers.append((re * re + im * im) * (1.0 / length))
                    level = jnp.sum(powers[0] + powers[1], axis=1, keepdims=True) * (1.0 / half)
                    floor = WATER * level + 1e-06
                    even, odd = jnp.log(powers[0] + floor), jnp.log(powers[1] + floor)
                    logs[at, :quarter] = even
                    logs[at, quarter:] = odd
                    we, wo = weigh(even, odd, present, first, last)
                    src_even = rcv_even = we * even
                    src_odd = rcv_odd = wo * odd
                else:
                    even, odd = logs[at, :quarter], logs[at, quarter:]
                    ue, uo = even - terms[i : i + 1, :quarter], odd - terms[i : i + 1, quarter:]
                    te, to = rcv_ref[:, :quarter], rcv_ref[:, quarter:]
                    we, wo = weigh(ue - te, uo - to, present, first, last)
                    src_even, src_odd = we * (even - te), wo * (odd - to)
                    rcv_even, rcv_odd = we * ue, wo * uo
                s_part[it, chunk, i : i + 1, :quarter] = jnp.sum(src_even, axis=0, keepdims=True)
                s_part[it, chunk, i : i + 1, quarter:] = jnp.sum(src_odd, axis=0, keepdims=True)
                s_part[it, chunk, ks + i : ks + i + 1, :quarter] = jnp.sum(we, axis=0, keepdims=True)
                s_part[it, chunk, ks + i : ks + i + 1, quarter:] = jnp.sum(wo, axis=0, keepdims=True)
                for q, value in enumerate((rcv_even, rcv_odd, we, wo)):
                    sums[q] = value if i == 0 else sums[q] + value
            for q in range(4):
                cols = slice((q % 2) * quarter, (q % 2 + 1) * quarter)
                kept = sums[q] if count == 0 else acc[it, q // 2, :, cols] + sums[q]
                acc[it, q // 2, :, cols] = kept
            if it == 0:
                at = slice(d * tile, (d + 1) * tile)
                stores.append(pltpu.make_async_copy(spec_ref.at[at], spec_hbm.at[at], out_sem.at[d]))
                stores[-1].start()
            if it == 0 and count == 0:
                pl.semaphore_wait(barrier, ns + nr - 2)
            if d < nr - 1:
                send(it, "rcv", chunk, d, s_part.at[it, chunk], s_recv.at[it, me_r], s_ssem, s_rsem, me_r)
        for p in range(ns):
            r_part[it, p, :kr, :] = acc[it, 0, p * kr : (p + 1) * kr, :]
            r_part[it, p, kr:, :] = acc[it, 1, p * kr : (p + 1) * kr, :]
        for d in range(1, ns):
            peer = lax.rem(me_s + d, ns)
            send(it, "src", peer, d, r_part.at[it, peer], r_recv.at[it, me_s], r_ssem, r_rsem, me_s)
        if it == 0:
            finish_src(it)
            finish_rcv(it)
        else:
            finish_rcv(it)
            finish_src(it)
        collect_rcv(it)
    loads[nr + 2].wait()
    arrive_all(it, "rcv", nr, me_r, s_gath, sg_ssem, sg_rsem)
    for p in range(nr):
        src_ref[p * ks : (p + 1) * ks, :] = s_gath[it, p]
    for copy in stores:
        copy.wait()
    for copy in sends:
        copy.wait_send()


def filter_kernel(
    rows, nr, mask_ref, count_ref, spec_hbm, src_ref, rcv_ref, inv_ref, out_hbm,
    spec_ref, upper, lower, stage, in_sem, sem,
):
    src_rows, rcv_rows = rows
    quarter = spec_ref.shape[1] // 4
    half = 2 * quarter
    ks = src_rows // nr
    tile = ks * rcv_rows
    order = far_first(lax.axis_index("rcv"), nr)
    limit = count_ref[0, 0] * jnp.where(mask_ref[0, 0] == 1, 1, 0)
    row = lax.broadcasted_iota(jnp.int32, (rcv_rows, quarter), 0)

    loads = []
    for d in range(nr):
        at = slice(d * tile, (d + 1) * tile)
        loads.append(pltpu.make_async_copy(spec_hbm.at[at], spec_ref.at[at], in_sem.at[d]))
        loads[d].start()

    def apply(d):
        loads[d].wait()
        terms = src_ref[pl.ds(pl.multiple_of(order[d] * ks, ks), ks), :]
        for i in range(ks):
            top = d * tile + i * rcv_rows
            at = slice(top, top + rcv_rows)
            alive = row + (order[d] * tile + i * rcv_rows) < limit
            for parity in (0, 1):
                cols = slice(parity * quarter, (parity + 1) * quarter)
                gain = jnp.exp(-0.5 * (terms[i : i + 1, cols] + rcv_ref[:, cols]))
                gain = jnp.where(alive, gain, 0.0)
                for part in (0, 1):
                    lo = parity * half + part * quarter
                    value = spec_ref[at, lo : lo + quarter] * gain
                    high = value.astype(BF16)
                    upper[at, lo : lo + quarter] = high
                    lower[at, lo : lo + quarter] = (value - high.astype(F32)).astype(BF16)

    def product(at, parity):
        cols = slice(parity * half, (parity + 1) * half)
        big, small = upper[at, cols], lower[at, cols]
        dot = functools.partial(jnp.dot, preferred_element_type=F32)
        return dot(big, inv_ref[parity]) + dot(small, inv_ref[parity]) + dot(big, inv_ref[2 + parity])

    copies = []
    apply(0)
    for d in range(nr):
        if d + 1 < nr:
            apply(d + 1)
        at = slice(d * tile, (d + 1) * tile)
        a, b = product(at, 0), product(at, 1)
        stage[at, :half] = a + b
        stage[at, half:] = a - b
        base = pl.multiple_of(order[d] * tile, tile)
        copy = pltpu.make_async_copy(stage.at[at], out_hbm.at[pl.ds(base, tile)], sem.at[d])
        copy.start()
        copies.append(copy)
    for copy in copies:
        copy.wait()


def kernel_body(ns, nr, traces, mask, count):
    src_rows, rcv_rows, length = traces.shape
    total, half = src_rows * rcv_rows, length // 2
    ks, kr = src_rows // nr, rcv_rows // ns
    forward_high, forward_low, inverse = kernel_tables(length)
    flat = traces.reshape(total, length)
    vmem = pl.BlockSpec(memory_space=pltpu.VMEM)
    smem = pl.BlockSpec(memory_space=pltpu.SMEM)
    hbm = pl.BlockSpec(memory_space=pltpu.HBM)
    dma = pltpu.SemaphoreType.DMA
    spectra, src_term, rcv_term, inverse = pl.pallas_call(
        functools.partial(sweep_kernel, (src_rows, rcv_rows), ns, nr),
        out_shape=(
            jax.ShapeDtypeStruct((total, length), F32),
            jax.ShapeDtypeStruct((src_rows, half), F32),
            jax.ShapeDtypeStruct((rcv_rows, half), F32),
            jax.ShapeDtypeStruct(inverse.shape, BF16),
        ),
        in_specs=[smem, smem, hbm, hbm, hbm, hbm],
        out_specs=(hbm, vmem, vmem, vmem),
        scratch_shapes=[
            pltpu.VMEM((total, length), F32),
            pltpu.VMEM((total, length), BF16),
            pltpu.VMEM((length, length), BF16),
            pltpu.VMEM((length, length), BF16),
            pltpu.VMEM((total, half), F32),
            pltpu.VMEM((ITERS, 2, rcv_rows, half), F32),
            pltpu.VMEM((ITERS, nr, 2 * ks, half), F32),
            pltpu.VMEM((ITERS, ns, 2 * kr, half), F32),
            pltpu.VMEM((ITERS, nr, 2 * ks, half), F32),
            pltpu.VMEM((ITERS, ns, 2 * kr, half), F32),
            pltpu.VMEM((ITERS, nr, ks, half), F32),
            pltpu.VMEM((ITERS, ns, kr, half), F32),
            dma((nr + 3,)),
            dma((nr,)),
            dma((ITERS, nr)), dma((ITERS, nr)), dma((ITERS, ns)), dma((ITERS, ns)),
            dma((ITERS, nr)), dma((ITERS, nr)), dma((ITERS, ns)), dma((ITERS, ns)),
        ],
        compiler_params=pltpu.CompilerParams(
            collective_id=0, has_side_effects=True, vmem_limit_bytes=VMEM_BYTES - ROOM
        ),
        name="sweeps",
    )(mask, count, flat, jnp.asarray(forward_high), jnp.asarray(forward_low), jnp.asarray(inverse))
    output = pl.pallas_call(
        functools.partial(filter_kernel, (src_rows, rcv_rows), nr),
        out_shape=jax.ShapeDtypeStruct((total, length), F32),
        in_specs=[smem, smem, hbm, vmem, vmem, vmem],
        out_specs=hbm,
        scratch_shapes=[
            pltpu.VMEM((total, length), F32),
            pltpu.VMEM((total, length), BF16),
            pltpu.VMEM((total, length), BF16),
            pltpu.VMEM((total, length), F32),
            dma((nr,)),
            dma((nr,)),
        ],
        compiler_params=pltpu.CompilerParams(vmem_limit_bytes=VMEM_BYTES - ROOM),
        name="filters",
    )(mask, count, spectra, src_term, rcv_term, inverse)
    return output.reshape(src_rows, rcv_rows, length)


def solution(mesh):
    ns, nr = mesh.shape["src"], mesh.shape["rcv"]

    def body(traces, mask, count):
        src_rows, rcv_rows, length = traces.shape
        fits = src_rows % (8 * nr) == 0 and rcv_rows % (4 * ns) == 0 and length % (4 * LANES) == 0
        if fits and ns > 1 and nr > 1:
            return kernel_body(ns, nr, traces, mask, count)
        return plain_body(traces, mask, count)

    return jax.shard_map(
        body,
        mesh=mesh,
        in_specs=(P("src", "rcv", None), P("src", "rcv"), P("src", "rcv")),
        out_specs=P("src", "rcv", None),
        check_vma=False,
    )
```
